256 devices in a mesh: gx: 16 (over z, core), gy: 4 (over x), member: 4 (over y).
Axes of the slice: x: 4, y: 4, z: 8, core: 2. Of those that a mesh axis runs over, the one named last changes fastest.
Arguments:
- density: float32 [4, 64, 128, 256], P('member', 'gx', 'gy'), may hold values from 0.5 to 1.5
- velocity: float32 [4, 3, 64, 128, 256], P('member', None, 'gx', 'gy'), may hold values from -0.5 to 0.5
- pressure: float32 [4, 64, 128, 256], P('member', 'gx', 'gy'), may hold values from 0.5 to 1.5
- start_block: float32 [4, 128, 16], P('member'), may hold values from -6 to 6
- test_vectors: float32 [32, 64, 128], P('gx', 'gy'), may hold values from -48 to 48
Outputs:
- state_next: float32 [4, 5, 64, 128, 256], P('member', None, 'gx', 'gy')
- projected: float32 [32, 64, 128], P('gx', 'gy')
The draws below stay inside these ranges and needn't reach their ends.
All inputs are finite; a program needn't handle non-finite values.
Results may differ from the reference program's by a relative error of at most 0.00013.
Values sent between devices are 32-bit elements; how exact they have to be, the bound alone decides.
A program may use at most 64 MiB of HBM per device.

```python
import jax
import jax.numpy as jnp
from jax import lax

NZ = 256
RANK = 16
NV = 128
MEMBERS = 4
NX = 64
NY = 128
SNAPS = 128


def levels(own_key, dims, cuts, smallest, top_value):
    gain, own = 1.0, jax.random.fold_in(own_key, 6)
    for axis_at, parts in cuts:
        heights = jnp.exp(jax.random.uniform(jax.random.fold_in(own, axis_at), (parts,), jnp.float32, smallest / len(cuts), top_value / len(cuts)))
        gain = gain * jnp.repeat(heights, dims[axis_at] // parts).reshape([-1 if axis == axis_at else 1 for axis in range(len(dims))])
    return gain


def scatter_about(rng, dims, width, reach, cuts=(), kind=jnp.bfloat16):
    entries = width * jax.random.normal(rng, dims, jnp.float32)
    if cuts:
        entries = entries * levels(rng, dims, cuts, -0.22, 0.18)
    return jnp.clip(entries, -reach, reach).astype(kind)


def setup_inputs(seed: int = 0) -> dict:
    arg_keys = jax.random.split(jax.random.key(seed), 6)
    density = jnp.clip(0.5 + 1.0 * jax.random.uniform(arg_keys[0], (MEMBERS, NX, NY, NZ), jnp.float32) ** levels(arg_keys[0], (MEMBERS, NX, NY, NZ), ((0, 4), (1, 16), (2, 4)), -0.2, 0.2), 0.5, 1.5)
    velocity = jnp.clip(jax.random.uniform(arg_keys[1], (MEMBERS, 3, NX, NY, NZ), jnp.float32, -0.5, 0.5) * levels(arg_keys[1], (MEMBERS, 3, NX, NY, NZ), ((0, 4), (2, 16), (3, 4)), -0.4, 0.0), -0.5, 0.5)
    pressure = jnp.clip(0.5 + 1.0 * jax.random.uniform(arg_keys[2], (MEMBERS, NX, NY, NZ), jnp.float32) ** levels(arg_keys[2], (MEMBERS, NX, NY, NZ), ((0, 4), (1, 16), (2, 4)), -0.2, 0.2), 0.5, 1.5)
    start_block = scatter_about(arg_keys[3], (MEMBERS, SNAPS, RANK), 1.0, 6.0, ((0, 4),), jnp.float32)
    test_vectors = scatter_about(arg_keys[4], (NX // 2, NY // 2, NV), 8.0, 48.0, ((0, 16), (1, 4)), jnp.float32)
    return {"density": density, "velocity": velocity, "pressure": pressure, "start_block": start_block, "test_vectors": test_vectors}


HEAT_RATIO = 1.4
TIME_STEP = 0.08
PRECISE = lax.Precision.HIGHEST

def cut(values, dimension, start_at, stop_at):
    return lax.slice_in_dim(values, start_at, stop_at, axis=dimension)

def conserved(density, velocity, pressure):
    momentum = density[None] * velocity
    energy = pressure / (HEAT_RATIO - 1.0) + 0.5 * density * lax.optimization_barrier(jnp.sum(velocity * velocity, axis=0))
    return jnp.concatenate([density[None], momentum, energy[None]], axis=0)

def primitive(fields):
    velocity = fields[1:4] / fields[0]
    kinetic = 0.5 * lax.optimization_barrier(jnp.sum(fields[1:4] * velocity, axis=0))
    pressure = (HEAT_RATIO - 1.0) * (fields[4] - kinetic)
    sound_speed = jnp.sqrt(HEAT_RATIO * pressure / fields[0])
    return (velocity, pressure, sound_speed)

def directed(fields, velocity, pressure, sound_speed, direction):
    normal = velocity[direction]
    components = [fields[1 + direction]]
    for component in range(3):
        moment_flux = fields[1 + component] * normal
        if component == direction:
            moment_flux = moment_flux + pressure
        components.append(moment_flux)
    components.append((fields[4] + pressure) * normal)
    return (jnp.stack(components), jnp.abs(normal) + sound_speed)

def tendency(fields):
    velocity, pressure, sound_speed = primitive(fields)
    summed = None
    for direction in range(3):
        fluxes, wave_speed = directed(fields, velocity, pressure, sound_speed, direction)
        if direction < 2:
            dimension = 1 + direction
            extent = fields.shape[dimension]
            left_flux = cut(fluxes, dimension, 0, extent - 1)
            right_flux = cut(fluxes, dimension, 1, extent)
            left_fields = cut(fields, dimension, 0, extent - 1)
            right_fields = cut(fields, dimension, 1, extent)
            bound_speed = jnp.maximum(cut(wave_speed, dimension - 1, 0, extent - 1), cut(wave_speed, dimension - 1, 1, extent))
        else:
            left_flux = fluxes
            right_flux = jnp.roll(fluxes, -1, axis=3)
            left_fields = fields
            right_fields = jnp.roll(fields, -1, axis=3)
            bound_speed = jnp.maximum(wave_speed, jnp.roll(wave_speed, -1, axis=2))
        face_flux = 0.5 * (left_flux + right_flux) - 0.5 * bound_speed * (right_fields - left_fields)
        if direction < 2:
            change = cut(face_flux, dimension, 1, extent - 1) - cut(face_flux, dimension, 0, extent - 2)
            cross_dim = 2 - direction
            change = cut(change, cross_dim, 1, change.shape[cross_dim] - 1)
        else:
            change = face_flux - jnp.roll(face_flux, 1, axis=3)
            change = change[:, 1:-1, 1:-1]
        summed = change if summed is None else summed + change
    return -summed

def wrapped(fields):
    return jnp.pad(fields, ((0, 0), (1, 1), (1, 1), (0, 0)), mode='wrap')

def snapshot(fields):
    sampled = fields[0, ::2, ::2, ::2]
    flattened = sampled.reshape(-1, sampled.shape[2])
    return flattened - lax.optimization_barrier(jnp.mean(flattened, axis=1, keepdims=True))

def reference(density, velocity, pressure, start_block, test_vectors):

    def member_window(inputs):
        member_density, member_velocity, member_pressure, member_start = inputs
        fields = conserved(member_density, member_velocity, member_pressure)
        section_one = fields + TIME_STEP * tendency(wrapped(fields))
        second = 0.5 * fields + 0.5 * (section_one + TIME_STEP * tendency(wrapped(section_one)))
        matrix = snapshot(second)
        sketch = jnp.dot(matrix, member_start, precision=PRECISE)
        folded = jnp.dot(matrix.T, sketch, precision=PRECISE)
        member_basis = jnp.dot(matrix, folded, precision=PRECISE)
        return (second, member_basis)
    states, bases = lax.map(member_window, (density, velocity, pressure, start_block))
    stacked = jnp.transpose(bases, (1, 0, 2)).reshape(bases.shape[1], bases.shape[0] * bases.shape[2])
    vectors = test_vectors.reshape(-1, test_vectors.shape[2])
    gram_matrix = jnp.dot(stacked.T, stacked, precision=PRECISE)
    cross_terms = jnp.dot(stacked.T, vectors, precision=PRECISE)
    factor = jnp.linalg.cholesky(gram_matrix)
    halfway = lax.linalg.triangular_solve(factor, cross_terms, left_side=True, lower=True)
    coefficients = lax.linalg.triangular_solve(factor, halfway, left_side=True, lower=True, transpose_a=True)
    projected = jnp.dot(stacked, coefficients, precision=PRECISE).reshape(test_vectors.shape)
    return (states, projected)
```

```python
import functools

import jax
import jax.numpy as jnp
from jax import lax
from jax.experimental import pallas as pl
from jax.experimental.pallas import tpu as pltpu
from jax.sharding import PartitionSpec as P

HEAT_RATIO = 1.4
TIME_STEP = 0.08
PRECISE = lax.Precision.HIGHEST
MESH = pl.DeviceIdType.MESH


def padded(block, sides, width):
    for axis, dim in sides:
        count = lax.axis_size(axis)
        forward = [(i, i + 1) for i in range(count - 1)]
        forward.append((count - 1, 0))
        backward = [(target, source) for source, target in forward]
        low = lax.ppermute(
            lax.slice_in_dim(block, block.shape[dim] - width, None, axis=dim), axis, forward
        )
        high = lax.ppermute(lax.slice_in_dim(block, 0, width, axis=dim), axis, backward)
        block = jnp.concatenate([low, block, high], axis=dim)
    return block


def cut(values, dimension, start_at, stop_at):
    return lax.slice_in_dim(values, start_at, stop_at, axis=dimension)


def conserved(density, velocity, pressure):
    momentum = density[None] * velocity
    energy = pressure / (HEAT_RATIO - 1.0) + 0.5 * density * jnp.sum(velocity * velocity, axis=0)
    return jnp.concatenate([density[None], momentum, energy[None]], axis=0)


def primitive(fields):
    velocity = fields[1:4] / fields[0]
    kinetic = 0.5 * jnp.sum(fields[1:4] * velocity, axis=0)
    pressure = (HEAT_RATIO - 1.0) * (fields[4] - kinetic)
    sound_speed = jnp.sqrt(HEAT_RATIO * pressure / fields[0])
    return (velocity, pressure, sound_speed)


def directed(fields, velocity, pressure, sound_speed, direction):
    normal = velocity[direction]
    components = [fields[1 + direction]]
    for component in range(3):
        moment_flux = fields[1 + component] * normal
        if component == direction:
            moment_flux = moment_flux + pressure
        components.append(moment_flux)
    components.append((fields[4] + pressure) * normal)
    return (jnp.stack(components), jnp.abs(normal) + sound_speed)


def tendency(fields):
    velocity, pressure, sound_speed = primitive(fields)
    summed = None
    for direction in range(3):
        fluxes, wave_speed = directed(fields, velocity, pressure, sound_speed, direction)
        if direction < 2:
            dimension = 1 + direction
            extent = fields.shape[dimension]
            left_flux = cut(fluxes, dimension, 0, extent - 1)
            right_flux = cut(fluxes, dimension, 1, extent)
            left_fields = cut(fields, dimension, 0, extent - 1)
            right_fields = cut(fields, dimension, 1, extent)
            bound_speed = jnp.maximum(
                cut(wave_speed, dimension - 1, 0, extent - 1),
                cut(wave_speed, dimension - 1, 1, extent),
            )
        else:
            left_flux = fluxes
            right_flux = jnp.roll(fluxes, -1, axis=3)
            left_fields = fields
            right_fields = jnp.roll(fields, -1, axis=3)
            bound_speed = jnp.maximum(wave_speed, jnp.roll(wave_speed, -1, axis=2))
        face_flux = 0.5 * (left_flux + right_flux) - 0.5 * bound_speed * (
            right_fields - left_fields
        )
        if direction < 2:
            change = cut(face_flux, dimension, 1, extent - 1) - cut(
                face_flux, dimension, 0, extent - 2
            )
            cross_dim = 2 - direction
            change = cut(change, cross_dim, 1, change.shape[cross_dim] - 1)
        else:
            change = face_flux - jnp.roll(face_flux, 1, axis=3)
            change = change[:, 1:-1, 1:-1]
        summed = change if summed is None else summed + change
    return -summed


def ghosted(fields):
    return padded(fields, (("gx", 1), ("gy", 2)), 1)


def dot_nt(left, right):
    return lax.dot_general(
        left, right, (((1,), (1,)), ((), ())), precision=PRECISE, preferred_element_type=jnp.float32
    )


def dot_nn(left, right):
    return lax.dot_general(
        left, right, (((1,), (0,)), ((), ())), precision=PRECISE, preferred_element_type=jnp.float32
    )


class Place:
    def __init__(self, nz, ny, nm):
        self.nz, self.ny, self.nm = nz, ny, nm
        self.gx = lax.axis_index("gx")
        self.gy = lax.axis_index("gy")
        self.m = lax.axis_index("member")
        self.z = self.gx // 2
        self.c = self.gx % 2
        self.plane_index = self.gy * 2 + self.c
        self.stack_index = self.m * 2 + self.c

    def in_plane(self, step):
        other = (self.plane_index + step) % (2 * self.ny)
        return other % 2, (2 * self.z + other % 2, other // 2, self.m)

    def along_z(self, step):
        return (2 * ((self.z + step) % self.nz) + self.c, self.gy, self.m)

    def in_stack(self, step):
        other = (self.stack_index + step) % (2 * self.nm)
        return (2 * self.z + other % 2, self.gy, other // 2)

    def same_cells(self, step):
        return (self.gx, self.gy, (self.m + step) % self.nm)

    def everyone(self):
        peers = [self.in_plane(step)[1] for step in range(1, 2 * self.ny)]
        peers += [self.along_z(step) for step in range(1, self.nz)]
        peers += [self.in_stack(step) for step in range(1, 2 * self.nm)]
        return peers


def push(src, dst, sems, step, device):
    copy = pltpu.make_async_remote_copy(
        src_ref=src,
        dst_ref=dst,
        send_sem=sems.at[0, step],
        recv_sem=sems.at[1, step],
        device_id=device,
        device_id_type=MESH,
    )
    copy.start()
    return copy


def total(buffer, count):
    values = [buffer[i] for i in range(count)]
    while len(values) > 1:
        pairs = [a + b for a, b in zip(values[::2], values[1::2])]
        values = pairs + ([values[-1]] if len(values) % 2 else [])
    return values[0]


def reduce_and_gather(place, halves, plane_buf, z_buf, stack_buf, sems):
    sent = []
    first = []
    for step in range(1, 2 * place.ny):
        core, device = place.in_plane(step)
        first.append(
            push(halves.at[core], plane_buf.at[place.plane_index], sems.at[0], step, device)
        )
    plane_buf[place.plane_index] = halves[place.c]
    for copy in first:
        copy.wait_recv()
    z_buf[place.z] = total(plane_buf, 2 * place.ny)
    second = [
        push(z_buf.at[place.z], z_buf.at[place.z], sems.at[1], step, place.along_z(step))
        for step in range(1, place.nz)
    ]
    for copy in second:
        copy.wait_recv()
    stack_buf[place.stack_index] = total(z_buf, place.nz)
    third = [
        push(
            stack_buf.at[place.stack_index],
            stack_buf.at[place.stack_index],
            sems.at[2],
            step,
            place.in_stack(step),
        )
        for step in range(1, 2 * place.nm)
    ]
    for copy in third:
        copy.wait_recv()
    sent = first + second + third
    return sent


def eliminate(gram, cross):
    size = gram.shape[0]
    rows = lax.broadcasted_iota(jnp.int32, (size, 1), 0)
    scale = jnp.ones((size, 1), jnp.float32)
    for k in range(size):
        inverse = 1.0 / gram[k : k + 1, k : k + 1]
        factor = jnp.where(rows == k, 0.0, gram[:, k : k + 1] * inverse)
        scale = jnp.where(rows == k, inverse, scale)
        cross = cross - factor * cross[k : k + 1]
        gram = gram - factor * gram[k : k + 1]
    return cross * scale


def pod_kernel(
    nz, ny, nm, sampled, block_t, vectors, out,
    matrix_all, fold_half, fold_plane, fold_z, fold_all, prod_half, prod_plane, prod_z, prod_all,
    sems, member_sems,
):
    place = Place(nz, ny, nm)
    rank = block_t.shape[0]
    barrier = pltpu.get_barrier_semaphore()
    peers = place.everyone()
    for device in peers:
        pl.semaphore_signal(barrier, inc=1, device_id=device, device_id_type=MESH)
    density = sampled[...]
    matrix = density - jnp.mean(density, axis=1, keepdims=True)
    matrix_all[place.m] = matrix
    fold = dot_nn(dot_nt(block_t[...], matrix), matrix)
    fold_half[0] = fold[:8]
    fold_half[1] = fold[8:]
    pl.semaphore_wait(barrier, len(peers))
    gathers = [
        push(
            matrix_all.at[place.m],
            matrix_all.at[place.m],
            member_sems,
            step,
            place.same_cells(step),
        )
        for step in range(1, nm)
    ]
    sent = reduce_and_gather(place, fold_half, fold_plane, fold_z, fold_all, sems.at[0])
    for copy in gathers:
        copy.wait_recv()
    bases_t = [
        dot_nt(jnp.concatenate([fold_all[2 * i], fold_all[2 * i + 1]], axis=0), matrix_all[i])
        for i in range(nm)
    ]
    stacked_t = jnp.concatenate(bases_t, axis=0)
    own = jnp.concatenate([fold_all[2 * place.m], fold_all[2 * place.m + 1]], axis=0)
    own_t = dot_nt(own, matrix)
    wide = jnp.concatenate(
        [stacked_t, jnp.zeros((128 - nm * rank, stacked_t.shape[1]), jnp.float32)], axis=0
    )
    gram_rows = dot_nt(own_t, wide)
    cross_rows = dot_nn(own_t, vectors[...])
    for core in range(2):
        prod_half[core, :, :128] = gram_rows[8 * core : 8 * core + 8]
        prod_half[core, :, 128:] = cross_rows[8 * core : 8 * core + 8]
    sent += reduce_and_gather(place, prod_half, prod_plane, prod_z, prod_all, sems.at[1])
    both = jnp.concatenate([prod_all[i] for i in range(2 * nm)], axis=0)
    weights = eliminate(both[:, :128], both[:, 128:])
    out[...] = dot_nn(stacked_t.T, weights)
    for copy in sent + gathers:
        copy.wait_send()


def pod(sampled, block_t, vectors, nz, ny, nm):
    slots = max(2 * ny, nz, 2 * nm)
    vmem = pl.BlockSpec(memory_space=pltpu.VMEM)
    f32 = jnp.float32
    return pl.pallas_call(
        functools.partial(pod_kernel, nz, ny, nm),
        out_shape=jax.ShapeDtypeStruct(vectors.shape, f32),
        in_specs=[vmem] * 3,
        out_specs=vmem,
        scratch_shapes=[
            pltpu.VMEM((nm, *sampled.shape), f32),
            pltpu.VMEM((2, 8, 128), f32),
            pltpu.VMEM((2 * ny, 8, 128), f32),
            pltpu.VMEM((nz, 8, 128), f32),
            pltpu.VMEM((2 * nm, 8, 128), f32),
            pltpu.VMEM((2, 8, 256), f32),
            pltpu.VMEM((2 * ny, 8, 256), f32),
            pltpu.VMEM((nz, 8, 256), f32),
            pltpu.VMEM((2 * nm, 8, 256), f32),
            pltpu.SemaphoreType.DMA((2, 3, 2, slots)),
            pltpu.SemaphoreType.DMA((2, nm)),
        ],
        compiler_params=pltpu.CompilerParams(collective_id=0, has_side_effects=True),
    )(sampled, block_t, vectors)


def shards(sizes, density, velocity, pressure, start_block, test_vectors):
    fields = conserved(density[0], velocity[0], pressure[0])
    section_one = fields + TIME_STEP * tendency(ghosted(fields))
    second = 0.5 * fields + 0.5 * (section_one + TIME_STEP * tendency(ghosted(section_one)))
    sampled = second[0, ::2, ::2, ::2]
    flattened = sampled.reshape(-1, sampled.shape[2])
    vectors = test_vectors.reshape(-1, test_vectors.shape[2])
    projected = pod(flattened, start_block[0].T, vectors, *sizes).reshape(test_vectors.shape)
    return (second[None], projected)


def solution(mesh):
    sizes = (mesh.shape["gx"] // 2, mesh.shape["gy"], mesh.shape["member"])
    return jax.shard_map(
        functools.partial(shards, sizes),
        mesh=mesh,
        in_specs=(
            P("member", "gx", "gy", None),
            P("member", None, "gx", "gy", None),
            P("member", "gx", "gy", None),
            P("member", None, None),
            P("gx", "gy", None),
        ),
        out_specs=(P("member", None, "gx", "gy", None), P("gx", "gy", None)),
        check_vma=False,
    )
```

```python
import functools

import jax
import jax.numpy as jnp
from jax import lax
from jax.experimental import pallas as pl
from jax.experimental.pallas import tpu as pltpu
from jax.sharding import PartitionSpec as P

HEAT_RATIO = 1.4
TIME_STEP = 0.08
HALF_STEP = 0.5 * TIME_STEP
PRECISE = lax.Precision.HIGHEST
MESH = pl.DeviceIdType.MESH

PLANES, ROWS, OWN_ROWS = 8, 40, 32
RHO, VEL, PRES, MOM, ENERGY, SOUND = 0, 1, 4, 5, 8, 9
CONSERVED = (RHO, MOM, MOM + 1, MOM + 2, ENERGY)


def dot_nt(left, right):
    return lax.dot_general(
        left, right, (((1,), (1,)), ((), ())), precision=PRECISE, preferred_element_type=jnp.float32
    )


def dot_nn(left, right):
    return lax.dot_general(
        left, right, (((1,), (0,)), ((), ())), precision=PRECISE, preferred_element_type=jnp.float32
    )


class Place:
    def __init__(self, nz, ny, nm):
        self.nz, self.ny, self.nm = nz, ny, nm
        self.gx = lax.axis_index("gx")
        self.gy = lax.axis_index("gy")
        self.m = lax.axis_index("member")
        self.z = self.gx // 2
        self.c = self.gx % 2
        self.plane_index = self.gy * 2 + self.c
        self.stack_index = self.m * 2 + self.c

    def neighbour(self, up_x, up_y):
        nx = 2 * self.nz
        return ((self.gx + up_x + nx) % nx, (self.gy + up_y + self.ny) % self.ny, self.m)

    def in_plane(self, step):
        other = (self.plane_index + step) % (2 * self.ny)
        return other % 2, (2 * self.z + other % 2, other // 2, self.m)

    def along_z(self, step):
        return (2 * ((self.z + step) % self.nz) + self.c, self.gy, self.m)

    def in_stack(self, step):
        other = (self.stack_index + step) % (2 * self.nm)
        return (2 * self.z + other % 2, self.gy, other // 2)

    def same_cells(self, step):
        return (self.gx, self.gy, (self.m + step) % self.nm)

    def everyone(self):
        peers = [self.neighbour(x, y) for x in (-1, 0, 1) for y in (-1, 0, 1) if (x, y) != (0, 0)]
        peers += [self.in_plane(step)[1] for step in range(1, 2 * self.ny)]
        peers += [self.along_z(step) for step in range(1, self.nz)]
        peers += [self.in_stack(step) for step in range(1, 2 * self.nm)]
        return peers


def push(src, dst, send_sem, recv_sem, device):
    copy = pltpu.make_async_remote_copy(
        src_ref=src,
        dst_ref=dst,
        send_sem=send_sem,
        recv_sem=recv_sem,
        device_id=device,
        device_id_type=MESH,
    )
    copy.start()
    return copy


def total(buffer, count):
    values = [buffer[i] for i in range(count)]
    while len(values) > 1:
        pairs = [a + b for a, b in zip(values[::2], values[1::2])]
        values = pairs + ([values[-1]] if len(values) % 2 else [])
    return values[0]


def reduce_and_gather(place, halves, plane_buf, z_buf, stack_buf, sems, meanwhile):
    first = []
    for step in range(1, 2 * place.ny):
        core, device = place.in_plane(step)
        first.append(
            push(
                halves.at[core],
                plane_buf.at[place.plane_index],
                sems.at[0, 0, step],
                sems.at[0, 1, step],
                device,
            )
        )
    plane_buf[place.plane_index] = halves[place.c]
    meanwhile[0]()
    for copy in first:
        copy.wait_recv()
    z_buf[place.z] = total(plane_buf, 2 * place.ny)
    second = [
        push(
            z_buf.at[place.z],
            z_buf.at[place.z],
            sems.at[1, 0, step],
            sems.at[1, 1, step],
            place.along_z(step),
        )
        for step in range(1, place.nz)
    ]
    meanwhile[1]()
    for copy in second:
        copy.wait_recv()
    stack_buf[place.stack_index] = total(z_buf, place.nz)
    third = [
        push(
            stack_buf.at[place.stack_index],
            stack_buf.at[place.stack_index],
            sems.at[2, 0, step],
            sems.at[2, 1, step],
            place.in_stack(step),
        )
        for step in range(1, 2 * place.nm)
    ]
    meanwhile[2]()
    for copy in third:
        copy.wait_recv()
    return first + second + third


def eliminate(gram, cross):
    size = gram.shape[0]
    rows = lax.broadcasted_iota(jnp.int32, (size, 1), 0)
    scale = jnp.ones((size, 1), jnp.float32)
    for k in range(size):
        inverse = 1.0 / gram[k : k + 1, k : k + 1]
        factor = jnp.where(rows == k, 0.0, gram[:, k : k + 1] * inverse)
        scale = jnp.where(rows == k, inverse, scale)
        cross = cross - factor * cross[k : k + 1]
        gram = gram - factor * gram[k : k + 1]
    return cross * scale


def ahead(values, axis):
    return pltpu.roll(values, values.shape[axis] - 1, axis)


def behind(values, axis):
    return pltpu.roll(values, 1, axis)


def flux(cells, plane, field, direction, pressure, normal):
    value = cells[field, plane]
    if field == RHO:
        return cells[MOM + direction, plane], value
    if field == ENERGY:
        return (value + pressure) * normal, value
    result = value * normal
    return (result + pressure if field == MOM + direction else result), value


def first_faces(cells, faces, plane, fields):
    low_v, high_v = cells[VEL, plane], cells[VEL, plane + 1]
    low_p, high_p = cells[PRES, plane], cells[PRES, plane + 1]
    speed = jnp.maximum(
        jnp.abs(low_v) + cells[SOUND, plane], jnp.abs(high_v) + cells[SOUND, plane + 1]
    )
    for field in fields:
        low_f, low_u = flux(cells, plane, field, 0, low_p, low_v)
        high_f, high_u = flux(cells, plane + 1, field, 0, high_p, high_v)
        faces[CONSERVED.index(field), plane] = (low_f + high_f) - speed * (high_u - low_u)


def changes(cells, faces, plane, fields):
    sums = [faces[CONSERVED.index(f), plane] - faces[CONSERVED.index(f), plane - 1] for f in fields]
    pressure, sound = cells[PRES, plane], cells[SOUND, plane]
    for direction in (1, 2):
        axis = direction - 1
        normal = cells[VEL + direction, plane]
        speed = jnp.abs(normal) + sound
        speed = jnp.maximum(speed, ahead(speed, axis))
        for at, field in enumerate(fields):
            here, value = flux(cells, plane, field, direction, pressure, normal)
            face = (here + ahead(here, axis)) - speed * (ahead(value, axis) - value)
            sums[at] = sums[at] + (face - behind(face, axis))
    return sums


def complete_initial(cells, plane, rows):
    rho, pressure = cells[RHO, plane, rows], cells[PRES, plane, rows]
    squares = None
    for k in range(3):
        velocity = cells[VEL + k, plane, rows]
        cells[MOM + k, plane, rows] = rho * velocity
        squares = velocity * velocity if squares is None else squares + velocity * velocity
    cells[ENERGY, plane, rows] = pressure * (1.0 / (HEAT_RATIO - 1.0)) + 0.5 * rho * squares
    cells[SOUND, plane, rows] = jnp.sqrt(HEAT_RATIO * pressure / rho)


def first_stage(cells, faces, after, plane):
    sums = changes(cells, faces, plane, CONSERVED)
    values = [cells[f, plane] - HALF_STEP * s for f, s in zip(CONSERVED, sums)]
    rho, energy = values[0], values[4]
    inverse = 1.0 / rho
    kinetic = None
    for k in range(3):
        velocity = values[1 + k] * inverse
        after[MOM + k, plane] = values[1 + k]
        after[VEL + k, plane] = velocity
        term = values[1 + k] * velocity
        kinetic = term if kinetic is None else kinetic + term
    pressure = (HEAT_RATIO - 1.0) * (energy - 0.5 * kinetic)
    after[RHO, plane] = rho
    after[ENERGY, plane] = energy
    after[PRES, plane] = pressure
    after[SOUND, plane] = jnp.sqrt(HEAT_RATIO * pressure * inverse)


def second_stage(cells, after, faces, result, plane, fields):
    sums = changes(after, faces, plane, fields)
    for field, s in zip(fields, sums):
        value = 0.5 * cells[field, plane] + 0.5 * (after[field, plane] - HALF_STEP * s)
        result[CONSERVED.index(field), plane - 2] = value[:OWN_ROWS]


def over(first, stop, body):
    lax.fori_loop(first, stop, lambda i, carry: (body(i), carry)[1], 0)


def window_kernel(
    nz, ny, nm, density, velocity, pressure, block, test, state, out,
    cells, after, faces, result, row_send, row_recv, corner_send, corner_recv, pick, thin,
    block_in, test_in,
    matrix_all, fold_half, fold_plane, fold_z, fold_all, prod_half, prod_plane, prod_z, prod_all,
    local_sems, halo_sems, sems, member_sems,
):
    place = Place(nz, ny, nm)
    rank = block.shape[2]
    snaps = block.shape[1]
    barrier = pltpu.get_barrier_semaphore()
    peers = place.everyone()
    own = pl.ds(0, OWN_ROWS)
    loads = [
        pltpu.make_async_copy(density.at[0], cells.at[RHO, 2:6, own], local_sems.at[0]),
        pltpu.make_async_copy(velocity.at[0], cells.at[VEL : VEL + 3, 2:6, own], local_sems.at[1]),
        pltpu.make_async_copy(pressure.at[0], cells.at[PRES, 2:6, own], local_sems.at[2]),
    ]
    late_loads = [
        pltpu.make_async_copy(block.at[0], block_in, local_sems.at[3]),
        pltpu.make_async_copy(test, test_in, local_sems.at[4]),
    ]
    for copy in loads + late_loads:
        copy.start()
    for device in peers:
        pl.semaphore_signal(barrier, inc=1, device_id=device, device_id_type=MESH)
    row = lax.broadcasted_iota(jnp.int32, pick.shape, 0)
    column = lax.broadcasted_iota(jnp.int32, pick.shape, 1)
    pick[...] = jnp.where(row == 2 * column, 1.0, 0.0) - jnp.where(row % 2 == 0, 1.0 / snaps, 0.0)
    for copy in loads:
        copy.wait()
    raw = slice(0, 5)
    for i in range(4):
        row_send[0, :, 2 * i : 2 * i + 2] = cells[raw, 2 + i, OWN_ROWS - 2 : OWN_ROWS]
        row_send[1, :, 2 * i : 2 * i + 2] = cells[raw, 2 + i, 0:2]
    corners = ((1, 1), (1, -1), (-1, 1), (-1, -1))
    for at, (up_x, up_y) in enumerate(corners):
        line = OWN_ROWS - 1 if up_y == 1 else 0
        for f in range(5):
            corner_send[at, f : f + 1] = cells[f, 5 if up_x == 1 else 2, line : line + 1]
    pl.semaphore_wait(barrier, len(peers))

    def plane_push(index, source, target, up_x):
        return push(
            cells.at[raw, source, own],
            cells.at[raw, target, own],
            halo_sems.at[0, index],
            halo_sems.at[1, index],
            place.neighbour(up_x, 0),
        )

    up_near, down_near = plane_push(0, 5, 1, 1), plane_push(1, 2, 6, -1)
    row_copies = [
        push(
            row_send.at[i],
            row_recv.at[i],
            halo_sems.at[0, 2 + i],
            halo_sems.at[1, 2 + i],
            place.neighbour(0, 1 - 2 * i),
        )
        for i in range(2)
    ]
    corner_copies = [
        push(
            corner_send.at[i],
            corner_recv.at[i],
            halo_sems.at[0, 4 + i],
            halo_sems.at[1, 4 + i],
            place.neighbour(*corners[i]),
        )
        for i in range(4)
    ]
    up_far, down_far = plane_push(8, 4, 0, 1), plane_push(9, 3, 7, -1)
    sent = [up_near, down_near, *row_copies, *corner_copies, up_far, down_far]

    over(2, 6, lambda p: complete_initial(cells, p, own))
    halo = pl.ds(OWN_ROWS, ROWS - OWN_ROWS)
    for copy in row_copies:
        copy.wait_recv()
    for i in range(4):
        cells[raw, 2 + i, ROWS - 2 : ROWS] = row_recv[0, :, 2 * i : 2 * i + 2]
        cells[raw, 2 + i, OWN_ROWS : OWN_ROWS + 2] = row_recv[1, :, 2 * i : 2 * i + 2]
    over(2, 6, lambda p: complete_initial(cells, p, halo))
    over(2, 5, lambda p: first_faces(cells, faces, p, CONSERVED))
    over(3, 5, lambda p: first_stage(cells, faces, after, p))

    for copy in corner_copies:
        copy.wait_recv()
    for at, (up_x, up_y) in enumerate(corners):
        line = ROWS - 1 if up_y == 1 else OWN_ROWS
        for f in range(5):
            cells[f, 1 if up_x == 1 else 6, line : line + 1] = corner_recv[at, f : f + 1]
    everything = pl.ds(0, ROWS)
    for copy, near, face, inner in ((down_near, 6, 5, 5), (up_near, 1, 1, 2)):
        copy.wait_recv()
        complete_initial(cells, near, everything)
        first_faces(cells, faces, face, CONSERVED)
        first_stage(cells, faces, after, inner)
    mass = (RHO,)
    rest = CONSERVED[1:]
    over(2, 5, lambda p: first_faces(after, faces, p, mass))
    second_stage(cells, after, faces, result, 4, mass)
    up_far.wait_recv()
    complete_initial(cells, 0, everything)
    first_faces(cells, faces, 0, CONSERVED)
    first_stage(cells, faces, after, 1)
    first_faces(after, faces, 1, mass)
    second_stage(cells, after, faces, result, 2, mass)

    even = pl.ds(0, OWN_ROWS // 2, stride=2)
    for i in range(2):
        for side in range(2):
            lanes = slice(128 * side, 128 * side + 128)
            thin[2 * i + side] = result[0, 2 * i, :, lanes]
    sampled = jnp.concatenate(
        [jnp.concatenate([thin[2 * i, even], thin[2 * i + 1, even]], axis=1) for i in range(2)],
        axis=0,
    )
    matrix = dot_nn(sampled, pick[...])
    matrix_all[place.m] = matrix
    for copy in late_loads:
        copy.wait()
    fold = dot_nn(dot_nt(block_in[...].T, matrix), matrix)
    fold_half[0] = fold[:8]
    fold_half[1] = fold[8:]
    gathers = [
        push(
            matrix_all.at[place.m],
            matrix_all.at[place.m],
            member_sems.at[0, step],
            member_sems.at[1, step],
            place.same_cells(step),
        )
        for step in range(1, nm)
    ]

    def last_plane():
        down_far.wait_recv()
        complete_initial(cells, 7, everything)
        first_faces(cells, faces, 6, CONSERVED)
        first_stage(cells, faces, after, 6)

    def other_fields():
        first_faces(after, faces, 5, mass)
        second_stage(cells, after, faces, result, 3, mass)
        second_stage(cells, after, faces, result, 5, mass)
        over(1, 6, lambda p: first_faces(after, faces, p, rest))
        over(2, 6, lambda p: second_stage(cells, after, faces, result, p, rest))

    store = pltpu.make_async_copy(result, state.at[0], local_sems.at[5])

    def nothing():
        pass

    sent += reduce_and_gather(
        place, fold_half, fold_plane, fold_z, fold_all, sems.at[0],
        (last_plane, other_fields, store.start),
    )
    for copy in gathers:
        copy.wait_recv()
    bases_t = [
        dot_nt(jnp.concatenate([fold_all[2 * i], fold_all[2 * i + 1]], axis=0), matrix_all[i])
        for i in range(nm)
    ]
    stacked_t = jnp.concatenate(bases_t, axis=0)
    own_fold = jnp.concatenate([fold_all[2 * place.m], fold_all[2 * place.m + 1]], axis=0)
    own_t = dot_nt(own_fold, matrix)
    wide = jnp.concatenate(
        [stacked_t, jnp.zeros((128 - nm * rank, stacked_t.shape[1]), jnp.float32)], axis=0
    )
    gram_rows = dot_nt(own_t, wide)
    vectors = jnp.concatenate([test_in[0], test_in[1]], axis=0)
    cross_rows = dot_nn(own_t, vectors)
    for core in range(2):
        prod_half[core, :, :128] = gram_rows[8 * core : 8 * core + 8]
        prod_half[core, :, 128:] = cross_rows[8 * core : 8 * core + 8]
    sent += reduce_and_gather(
        place, prod_half, prod_plane, prod_z, prod_all, sems.at[1], (nothing, nothing, nothing)
    )
    both = jnp.concatenate([prod_all[i] for i in range(2 * nm)], axis=0)
    weights = eliminate(both[:, :128], both[:, 128:])
    projected = dot_nn(stacked_t.T, weights)
    half = projected.shape[0] // 2
    out[0] = projected[:half]
    out[1] = projected[half:]
    store.wait()
    for copy in sent + gathers:
        copy.wait_send()


def shards(sizes, density, velocity, pressure, start_block, test_vectors):
    nz, ny, nm = sizes
    slots = max(2 * ny, nz, 2 * nm)
    anywhere = pl.BlockSpec(memory_space=pl.ANY)
    f32 = jnp.float32
    samples = test_vectors.shape[0] * test_vectors.shape[1]
    return pl.pallas_call(
        functools.partial(window_kernel, nz, ny, nm),
        out_shape=(
            jax.ShapeDtypeStruct((1, 5, *density.shape[1:]), f32),
            jax.ShapeDtypeStruct(test_vectors.shape, f32),
        ),
        in_specs=[anywhere] * 5,
        out_specs=(anywhere, pl.BlockSpec(memory_space=pltpu.VMEM)),
        scratch_shapes=[
            pltpu.VMEM((10, PLANES, ROWS, 256), f32),
            pltpu.VMEM((10, PLANES, ROWS, 256), f32),
            pltpu.VMEM((5, PLANES, ROWS, 256), f32),
            pltpu.VMEM((5, 4, OWN_ROWS, 256), f32),
            pltpu.VMEM((2, 5, 8, 256), f32),
            pltpu.VMEM((2, 5, 8, 256), f32),
            pltpu.VMEM((4, 8, 256), f32),
            pltpu.VMEM((4, 8, 256), f32),
            pltpu.VMEM((256, 128), f32),
            pltpu.VMEM((4, OWN_ROWS, 128), f32),
            pltpu.VMEM(start_block.shape[1:], f32),
            pltpu.VMEM(test_vectors.shape, f32),
            pltpu.VMEM((nm, samples, 128), f32),
            pltpu.VMEM((2, 8, 128), f32),
            pltpu.VMEM((2 * ny, 8, 128), f32),
            pltpu.VMEM((nz, 8, 128), f32),
            pltpu.VMEM((2 * nm, 8, 128), f32),
            pltpu.VMEM((2, 8, 256), f32),
            pltpu.VMEM((2 * ny, 8, 256), f32),
            pltpu.VMEM((nz, 8, 256), f32),
            pltpu.VMEM((2 * nm, 8, 256), f32),
            pltpu.SemaphoreType.DMA((6,)),
            pltpu.SemaphoreType.DMA((2, 10)),
            pltpu.SemaphoreType.DMA((2, 3, 2, slots)),
            pltpu.SemaphoreType.DMA((2, nm)),
        ],
        compiler_params=pltpu.CompilerParams(
            collective_id=0, has_side_effects=True, vmem_limit_bytes=48 * 1024 * 1024
        ),
    )(density, velocity, pressure, start_block, test_vectors)


def solution(mesh):
    sizes = (mesh.shape["gx"] // 2, mesh.shape["gy"], mesh.shape["member"])
    return jax.shard_map(
        functools.partial(shards, sizes),
        mesh=mesh,
        in_specs=(
            P("member", "gx", "gy", None),
            P("member", None, "gx", "gy", None),
            P("member", "gx", "gy", None),
            P("member", None, None),
            P("gx", "gy", None),
        ),
        out_specs=(P("member", None, "gx", "gy", None), P("gx", "gy", None)),
        check_vma=False,
    )
```

```python
import functools

import jax
import jax.numpy as jnp
from jax import lax
from jax.experimental import pallas as pl
from jax.experimental.pallas import tpu as pltpu
from jax.sharding import PartitionSpec as P

HEAT_RATIO = 1.4
TIME_STEP = 0.08
HALF_STEP = 0.5 * TIME_STEP
PRECISE = lax.Precision.HIGHEST
MESH = pl.DeviceIdType.MESH

PLANES, ROWS, OWN_ROWS = 8, 40, 32
RHO, VEL, PRES, MOM, ENERGY, SOUND = 0, 1, 4, 5, 8, 9
CONSERVED = (RHO, MOM, MOM + 1, MOM + 2, ENERGY)


def dot_nt(left, right):
    return lax.dot_general(
        left, right, (((1,), (1,)), ((), ())), precision=PRECISE, preferred_element_type=jnp.float32
    )


def dot_nn(left, right):
    return lax.dot_general(
        left, right, (((1,), (0,)), ((), ())), precision=PRECISE, preferred_element_type=jnp.float32
    )


class Place:
    def __init__(self, nz, ny, nm):
        self.nz, self.ny, self.nm = nz, ny, nm
        self.gx = lax.axis_index("gx")
        self.gy = lax.axis_index("gy")
        self.m = lax.axis_index("member")
        self.z = self.gx // 2
        self.c = self.gx % 2
        self.plane_index = self.gy * 2 + self.c
        self.stack_index = self.m * 2 + self.c

    def neighbour(self, up_x, up_y):
        nx = 2 * self.nz
        return ((self.gx + up_x + nx) % nx, (self.gy + up_y + self.ny) % self.ny, self.m)

    def in_plane(self, step):
        other = (self.plane_index + step) % (2 * self.ny)
        return other % 2, (2 * self.z + other % 2, other // 2, self.m)

    def along_z(self, step):
        return (2 * ((self.z + step) % self.nz) + self.c, self.gy, self.m)

    def in_stack(self, step):
        other = (self.stack_index + step) % (2 * self.nm)
        return (2 * self.z + other % 2, self.gy, other // 2)

    def same_cells(self, step):
        return (self.gx, self.gy, (self.m + step) % self.nm)

    def everyone(self):
        peers = [self.neighbour(x, y) for x in (-1, 0, 1) for y in (-1, 0, 1) if (x, y) != (0, 0)]
        peers += [self.in_plane(step)[1] for step in range(1, 2 * self.ny)]
        peers += [self.along_z(step) for step in range(1, self.nz)]
        peers += [self.in_stack(step) for step in range(1, 2 * self.nm)]
        return peers


def push(src, dst, send_sem, recv_sem, device):
    copy = pltpu.make_async_remote_copy(
        src_ref=src,
        dst_ref=dst,
        send_sem=send_sem,
        recv_sem=recv_sem,
        device_id=device,
        device_id_type=MESH,
    )
    copy.start()
    return copy


def total(buffer, count):
    values = [buffer[i] for i in range(count)]
    while len(values) > 1:
        pairs = [a + b for a, b in zip(values[::2], values[1::2])]
        values = pairs + ([values[-1]] if len(values) % 2 else [])
    return values[0]


def reduce_and_gather(place, halves, plane_buf, z_buf, stack_buf, sems, meanwhile):
    first = []
    for step in range(1, 2 * place.ny):
        core, device = place.in_plane(step)
        first.append(
            push(
                halves.at[core],
                plane_buf.at[place.plane_index],
                sems.at[0, 0, step],
                sems.at[0, 1, step],
                device,
            )
        )
    plane_buf[place.plane_index] = halves[place.c]
    meanwhile[0]()
    for copy in first:
        copy.wait_recv()
    z_buf[place.z] = total(plane_buf, 2 * place.ny)
    second = [
        push(
            z_buf.at[place.z],
            z_buf.at[place.z],
            sems.at[1, 0, step],
            sems.at[1, 1, step],
            place.along_z(step),
        )
        for step in range(1, place.nz)
    ]
    meanwhile[1]()
    for copy in second:
        copy.wait_recv()
    stack_buf[place.stack_index] = total(z_buf, place.nz)
    third = [
        push(
            stack_buf.at[place.stack_index],
            stack_buf.at[place.stack_index],
            sems.at[2, 0, step],
            sems.at[2, 1, step],
            place.in_stack(step),
        )
        for step in range(1, 2 * place.nm)
    ]
    meanwhile[2]()
    for copy in third:
        copy.wait_recv()
    return first + second + third


def eliminate(gram, cross):
    size = gram.shape[0]
    rows = lax.broadcasted_iota(jnp.int32, (size, 1), 0)
    scale = jnp.ones((size, 1), jnp.float32)
    for k in range(size):
        inverse = 1.0 / gram[k : k + 1, k : k + 1]
        factor = jnp.where(rows == k, 0.0, gram[:, k : k + 1] * inverse)
        scale = jnp.where(rows == k, inverse, scale)
        cross = cross - factor * cross[k : k + 1]
        gram = gram - factor * gram[k : k + 1]
    return cross * scale


def ahead(values, axis):
    return pltpu.roll(values, values.shape[axis] - 1, axis)


def behind(values, axis):
    return pltpu.roll(values, 1, axis)


def flux(cells, plane, field, direction, pressure, normal):
    value = cells[field, plane]
    if field == RHO:
        return cells[MOM + direction, plane], value
    if field == ENERGY:
        return (value + pressure) * normal, value
    result = value * normal
    return (result + pressure if field == MOM + direction else result), value


def first_faces(cells, faces, plane, fields):
    low_v, high_v = cells[VEL, plane], cells[VEL, plane + 1]
    low_p, high_p = cells[PRES, plane], cells[PRES, plane + 1]
    speed = jnp.maximum(
        jnp.abs(low_v) + cells[SOUND, plane], jnp.abs(high_v) + cells[SOUND, plane + 1]
    )
    for field in fields:
        low_f, low_u = flux(cells, plane, field, 0, low_p, low_v)
        high_f, high_u = flux(cells, plane + 1, field, 0, high_p, high_v)
        faces[CONSERVED.index(field), plane] = (low_f + high_f) - speed * (high_u - low_u)


def changes(cells, faces, plane, fields):
    sums = [faces[CONSERVED.index(f), plane] - faces[CONSERVED.index(f), plane - 1] for f in fields]
    pressure, sound = cells[PRES, plane], cells[SOUND, plane]
    for direction in (1, 2):
        axis = direction - 1
        normal = cells[VEL + direction, plane]
        speed = jnp.abs(normal) + sound
        speed = jnp.maximum(speed, ahead(speed, axis))
        for at, field in enumerate(fields):
            here, value = flux(cells, plane, field, direction, pressure, normal)
            face = (here + ahead(here, axis)) - speed * (ahead(value, axis) - value)
            sums[at] = sums[at] + (face - behind(face, axis))
    return sums


def complete_initial(cells, plane, rows):
    rho, pressure = cells[RHO, plane, rows], cells[PRES, plane, rows]
    squares = None
    for k in range(3):
        velocity = cells[VEL + k, plane, rows]
        cells[MOM + k, plane, rows] = rho * velocity
        squares = velocity * velocity if squares is None else squares + velocity * velocity
    cells[ENERGY, plane, rows] = pressure * (1.0 / (HEAT_RATIO - 1.0)) + 0.5 * rho * squares
    cells[SOUND, plane, rows] = jnp.sqrt(HEAT_RATIO * pressure / rho)


def first_stage(cells, faces, after, plane):
    sums = changes(cells, faces, plane, CONSERVED)
    values = [cells[f, plane] - HALF_STEP * s for f, s in zip(CONSERVED, sums)]
    rho, energy = values[0], values[4]
    inverse = 1.0 / rho
    kinetic = None
    for k in range(3):
        velocity = values[1 + k] * inverse
        after[MOM + k, plane] = values[1 + k]
        after[VEL + k, plane] = velocity
        term = values[1 + k] * velocity
        kinetic = term if kinetic is None else kinetic + term
    pressure = (HEAT_RATIO - 1.0) * (energy - 0.5 * kinetic)
    after[RHO, plane] = rho
    after[ENERGY, plane] = energy
    after[PRES, plane] = pressure
    after[SOUND, plane] = jnp.sqrt(HEAT_RATIO * pressure * inverse)


def second_stage(cells, after, faces, result, plane, fields):
    sums = changes(after, faces, plane, fields)
    for field, s in zip(fields, sums):
        value = 0.5 * cells[field, plane] + 0.5 * (after[field, plane] - HALF_STEP * s)
        result[CONSERVED.index(field), plane - 2] = value[:OWN_ROWS]


def over(first, stop, body):
    lax.fori_loop(first, stop, lambda i, carry: (body(i), carry)[1], 0)


def window_kernel(
    nz, ny, nm, density, velocity, pressure, block, test, state, out,
    cells, after, faces, result, row_send, row_recv, corner_send, corner_recv, pick, thin,
    block_in, test_in,
    matrix_all, fold_half, fold_plane, fold_z, fold_all, prod_half, prod_plane, prod_z, prod_all,
    local_sems, halo_sems, sems, member_sems,
):
    place = Place(nz, ny, nm)
    rank, snaps = block.shape[1:]
    barrier = pltpu.get_barrier_semaphore()
    peers = place.everyone()
    own = pl.ds(0, OWN_ROWS)
    loads = [
        pltpu.make_async_copy(density.at[0], cells.at[RHO, 2:6, own], local_sems.at[0]),
        pltpu.make_async_copy(velocity.at[0], cells.at[VEL : VEL + 3, 2:6, own], local_sems.at[1]),
        pltpu.make_async_copy(pressure.at[0], cells.at[PRES, 2:6, own], local_sems.at[2]),
    ]
    late_loads = [
        pltpu.make_async_copy(block.at[0], block_in, local_sems.at[3]),
        pltpu.make_async_copy(test, test_in, local_sems.at[4]),
    ]
    for copy in loads + late_loads:
        copy.start()
    for device in peers:
        pl.semaphore_signal(barrier, inc=1, device_id=device, device_id_type=MESH)
    row = lax.broadcasted_iota(jnp.int32, pick.shape, 0)
    column = lax.broadcasted_iota(jnp.int32, pick.shape, 1)
    pick[...] = jnp.where(row == 2 * column, 1.0, 0.0) - jnp.where(row % 2 == 0, 1.0 / snaps, 0.0)
    for copy in loads:
        copy.wait()
    raw = slice(0, 5)
    for i in range(4):
        row_send[0, :, 2 * i : 2 * i + 2] = cells[raw, 2 + i, OWN_ROWS - 2 : OWN_ROWS]
        row_send[1, :, 2 * i : 2 * i + 2] = cells[raw, 2 + i, 0:2]
    corners = ((1, 1), (1, -1), (-1, 1), (-1, -1))
    for at, (up_x, up_y) in enumerate(corners):
        line = OWN_ROWS - 1 if up_y == 1 else 0
        for f in range(5):
            corner_send[at, f : f + 1] = cells[f, 5 if up_x == 1 else 2, line : line + 1]
    pl.semaphore_wait(barrier, len(peers))

    def plane_push(index, source, target, up_x):
        return push(
            cells.at[raw, source, own],
            cells.at[raw, target, own],
            halo_sems.at[0, index],
            halo_sems.at[1, index],
            place.neighbour(up_x, 0),
        )

    up_near, down_near = plane_push(0, 5, 1, 1), plane_push(1, 2, 6, -1)
    row_copies = [
        push(
            row_send.at[i],
            row_recv.at[i],
            halo_sems.at[0, 2 + i],
            halo_sems.at[1, 2 + i],
            place.neighbour(0, 1 - 2 * i),
        )
        for i in range(2)
    ]
    corner_copies = [
        push(
            corner_send.at[i],
            corner_recv.at[i],
            halo_sems.at[0, 4 + i],
            halo_sems.at[1, 4 + i],
            place.neighbour(*corners[i]),
        )
        for i in range(4)
    ]
    up_far, down_far = plane_push(8, 4, 0, 1), plane_push(9, 3, 7, -1)
    sent = [up_near, down_near, *row_copies, *corner_copies, up_far, down_far]

    over(2, 6, lambda p: complete_initial(cells, p, own))
    halo = pl.ds(OWN_ROWS, ROWS - OWN_ROWS)
    for copy in row_copies:
        copy.wait_recv()
    for i in range(4):
        cells[raw, 2 + i, ROWS - 2 : ROWS] = row_recv[0, :, 2 * i : 2 * i + 2]
        cells[raw, 2 + i, OWN_ROWS : OWN_ROWS + 2] = row_recv[1, :, 2 * i : 2 * i + 2]
    over(2, 6, lambda p: complete_initial(cells, p, halo))
    over(2, 5, lambda p: first_faces(cells, faces, p, CONSERVED))
    over(3, 5, lambda p: first_stage(cells, faces, after, p))

    for copy in corner_copies:
        copy.wait_recv()
    for at, (up_x, up_y) in enumerate(corners):
        line = ROWS - 1 if up_y == 1 else OWN_ROWS
        for f in range(5):
            cells[f, 1 if up_x == 1 else 6, line : line + 1] = corner_recv[at, f : f + 1]
    everything = pl.ds(0, ROWS)
    for copy, near, face, inner in ((down_near, 6, 5, 5), (up_near, 1, 1, 2)):
        copy.wait_recv()
        complete_initial(cells, near, everything)
        first_faces(cells, faces, face, CONSERVED)
        first_stage(cells, faces, after, inner)
    mass = (RHO,)
    rest = CONSERVED[1:]
    over(2, 5, lambda p: first_faces(after, faces, p, mass))
    second_stage(cells, after, faces, result, 4, mass)
    up_far.wait_recv()
    complete_initial(cells, 0, everything)
    first_faces(cells, faces, 0, CONSERVED)
    first_stage(cells, faces, after, 1)
    first_faces(after, faces, 1, mass)
    second_stage(cells, after, faces, result, 2, mass)

    even = pl.ds(0, OWN_ROWS // 2, stride=2)
    for i in range(2):
        for side in range(2):
            lanes = slice(128 * side, 128 * side + 128)
            thin[2 * i + side] = result[0, 2 * i, :, lanes]
    sampled = jnp.concatenate(
        [jnp.concatenate([thin[2 * i, even], thin[2 * i + 1, even]], axis=1) for i in range(2)],
        axis=0,
    )
    matrix = dot_nn(sampled, pick[...])
    matrix_all[place.m] = matrix
    for copy in late_loads:
        copy.wait()
    fold = dot_nn(dot_nt(block_in[...], matrix), matrix)
    fold_half[0] = fold[:8]
    fold_half[1] = fold[8:]
    gathers = [
        push(
            matrix_all.at[place.m],
            matrix_all.at[place.m],
            member_sems.at[0, step],
            member_sems.at[1, step],
            place.same_cells(step),
        )
        for step in range(1, nm)
    ]

    def last_plane():
        down_far.wait_recv()
        complete_initial(cells, 7, everything)
        first_faces(cells, faces, 6, CONSERVED)
        first_stage(cells, faces, after, 6)

    def other_fields():
        first_faces(after, faces, 5, mass)
        second_stage(cells, after, faces, result, 3, mass)
        second_stage(cells, after, faces, result, 5, mass)
        over(1, 6, lambda p: first_faces(after, faces, p, rest))
        over(2, 6, lambda p: second_stage(cells, after, faces, result, p, rest))

    store = pltpu.make_async_copy(result, state.at[0], local_sems.at[5])

    def nothing():
        pass

    sent += reduce_and_gather(
        place, fold_half, fold_plane, fold_z, fold_all, sems.at[0],
        (last_plane, other_fields, store.start),
    )
    for copy in gathers:
        copy.wait_recv()
    bases_t = [
        dot_nt(jnp.concatenate([fold_all[2 * i], fold_all[2 * i + 1]], axis=0), matrix_all[i])
        for i in range(nm)
    ]
    stacked_t = jnp.concatenate(bases_t, axis=0)
    own_fold = jnp.concatenate([fold_all[2 * place.m], fold_all[2 * place.m + 1]], axis=0)
    own_t = dot_nt(own_fold, matrix)
    wide = jnp.concatenate(
        [stacked_t, jnp.zeros((128 - nm * rank, stacked_t.shape[1]), jnp.float32)], axis=0
    )
    gram_rows = dot_nt(own_t, wide)
    vectors = jnp.concatenate([test_in[0], test_in[1]], axis=0)
    cross_rows = dot_nn(own_t, vectors)
    for core in range(2):
        prod_half[core, :, :128] = gram_rows[8 * core : 8 * core + 8]
        prod_half[core, :, 128:] = cross_rows[8 * core : 8 * core + 8]
    sent += reduce_and_gather(
        place, prod_half, prod_plane, prod_z, prod_all, sems.at[1], (nothing, nothing, nothing)
    )
    both = jnp.concatenate([prod_all[i] for i in range(2 * nm)], axis=0)
    weights = eliminate(both[:, :128], both[:, 128:])
    projected = dot_nn(stacked_t.T, weights)
    half = projected.shape[0] // 2
    out[0] = projected[:half]
    out[1] = projected[half:]
    store.wait()
    for copy in sent + gathers:
        copy.wait_send()


def shards(sizes, density, velocity, pressure, start_block, test_vectors):
    nz, ny, nm = sizes
    slots = max(2 * ny, nz, 2 * nm)
    in_hbm = pl.BlockSpec(memory_space=pltpu.HBM)
    f32 = jnp.float32
    block_t = jnp.swapaxes(start_block, 1, 2)
    samples = test_vectors.shape[0] * test_vectors.shape[1]
    return pl.pallas_call(
        functools.partial(window_kernel, nz, ny, nm),
        out_shape=(
            jax.ShapeDtypeStruct((1, 5, *density.shape[1:]), f32),
            jax.ShapeDtypeStruct(test_vectors.shape, f32),
        ),
        in_specs=[in_hbm] * 5,
        out_specs=(in_hbm, pl.BlockSpec(memory_space=pltpu.VMEM)),
        scratch_shapes=[
            pltpu.VMEM((10, PLANES, ROWS, 256), f32),
            pltpu.VMEM((10, PLANES, ROWS, 256), f32),
            pltpu.VMEM((5, PLANES, ROWS, 256), f32),
            pltpu.VMEM((5, 4, OWN_ROWS, 256), f32),
            pltpu.VMEM((2, 5, 8, 256), f32),
            pltpu.VMEM((2, 5, 8, 256), f32),
            pltpu.VMEM((4, 8, 256), f32),
            pltpu.VMEM((4, 8, 256), f32),
            pltpu.VMEM((256, 128), f32),
            pltpu.VMEM((4, OWN_ROWS, 128), f32),
            pltpu.VMEM(block_t.shape[1:], f32),
            pltpu.VMEM(test_vectors.shape, f32),
            pltpu.VMEM((nm, samples, 128), f32),
            pltpu.VMEM((2, 8, 128), f32),
            pltpu.VMEM((2 * ny, 8, 128), f32),
            pltpu.VMEM((nz, 8, 128), f32),
            pltpu.VMEM((2 * nm, 8, 128), f32),
            pltpu.VMEM((2, 8, 256), f32),
            pltpu.VMEM((2 * ny, 8, 256), f32),
            pltpu.VMEM((nz, 8, 256), f32),
            pltpu.VMEM((2 * nm, 8, 256), f32),
            pltpu.SemaphoreType.DMA((6,)),
            pltpu.SemaphoreType.DMA((2, 10)),
            pltpu.SemaphoreType.DMA((2, 3, 2, slots)),
            pltpu.SemaphoreType.DMA((2, nm)),
        ],
        compiler_params=pltpu.CompilerParams(
            collective_id=0, has_side_effects=True, vmem_limit_bytes=48 * 1024 * 1024
        ),
    )(density, velocity, pressure, block_t, test_vectors)


def solution(mesh):
    sizes = (mesh.shape["gx"] // 2, mesh.shape["gy"], mesh.shape["member"])
    return jax.shard_map(
        functools.partial(shards, sizes),
        mesh=mesh,
        in_specs=(
            P("member", "gx", "gy", None),
            P("member", None, "gx", "gy", None),
            P("member", "gx", "gy", None),
            P("member", None, None),
            P("gx", "gy", None),
        ),
        out_specs=(P("member", None, "gx", "gy", None), P("gx", "gy", None)),
        check_vma=False,
    )
```

```python
import functools

import jax
import jax.numpy as jnp
from jax import lax
from jax.experimental import pallas as pl
from jax.experimental.pallas import tpu as pltpu
from jax.sharding import PartitionSpec as P

HEAT_RATIO = 1.4
TIME_STEP = 0.08
HALF_STEP = 0.5 * TIME_STEP
PRECISE = lax.Precision.HIGHEST
MESH = pl.DeviceIdType.MESH

PLANES, ROWS, OWN_ROWS = 8, 40, 32
RHO, VEL, PRES, MOM, ENERGY, SOUND = 0, 1, 4, 5, 8, 9
CONSERVED = (RHO, MOM, MOM + 1, MOM + 2, ENERGY)


def dot_nt(left, right):
    return lax.dot_general(
        left, right, (((1,), (1,)), ((), ())), precision=PRECISE, preferred_element_type=jnp.float32
    )


def dot_nn(left, right):
    return lax.dot_general(
        left, right, (((1,), (0,)), ((), ())), precision=PRECISE, preferred_element_type=jnp.float32
    )


class Place:
    def __init__(self, nz, ny, nm):
        self.nz, self.ny, self.nm = nz, ny, nm
        self.gx = lax.axis_index("gx")
        self.gy = lax.axis_index("gy")
        self.m = lax.axis_index("member")
        self.z = self.gx // 2
        self.c = self.gx % 2
        self.plane_index = self.gy * 2 + self.c
        self.stack_index = self.m * 2 + self.c

    def neighbour(self, up_x, up_y):
        nx = 2 * self.nz
        return ((self.gx + up_x + nx) % nx, (self.gy + up_y + self.ny) % self.ny, self.m)

    def in_plane(self, step):
        other = (self.plane_index + step) % (2 * self.ny)
        return other % 2, (2 * self.z + other % 2, other // 2, self.m)

    def along_z(self, step):
        return (2 * ((self.z + step) % self.nz) + self.c, self.gy, self.m)

    def in_stack(self, step):
        other = (self.stack_index + step) % (2 * self.nm)
        return (2 * self.z + other % 2, self.gy, other // 2)

    def same_cells(self, step):
        return (self.gx, self.gy, (self.m + step) % self.nm)

    def everyone(self):
        peers = [self.neighbour(x, y) for x in (-1, 0, 1) for y in (-1, 0, 1) if (x, y) != (0, 0)]
        peers += [self.in_plane(step)[1] for step in range(1, 2 * self.ny)]
        peers += [self.along_z(step) for step in range(1, self.nz)]
        peers += [self.in_stack(step) for step in range(1, 2 * self.nm)]
        return peers


def push(src, dst, send_sem, recv_sem, device):
    copy = pltpu.make_async_remote_copy(
        src_ref=src,
        dst_ref=dst,
        send_sem=send_sem,
        recv_sem=recv_sem,
        device_id=device,
        device_id_type=MESH,
    )
    copy.start()
    return copy


def total(buffer, count):
    values = [buffer[i] for i in range(count)]
    while len(values) > 1:
        pairs = [a + b for a, b in zip(values[::2], values[1::2])]
        values = pairs + ([values[-1]] if len(values) % 2 else [])
    return values[0]


def reduce_and_gather(place, halves, plane_buf, z_buf, stack_buf, sems, meanwhile):
    first = []
    for step in range(1, 2 * place.ny):
        core, device = place.in_plane(step)
        first.append(
            push(
                halves.at[core],
                plane_buf.at[place.plane_index],
                sems.at[0, 0, step],
                sems.at[0, 1, step],
                device,
            )
        )
    plane_buf[place.plane_index] = halves[place.c]
    meanwhile[0]()
    for copy in first:
        copy.wait_recv()
    z_buf[place.z] = total(plane_buf, 2 * place.ny)
    second = [
        push(
            z_buf.at[place.z],
            z_buf.at[place.z],
            sems.at[1, 0, step],
            sems.at[1, 1, step],
            place.along_z(step),
        )
        for step in range(1, place.nz)
    ]
    meanwhile[1]()
    for copy in second:
        copy.wait_recv()
    stack_buf[place.stack_index] = total(z_buf, place.nz)
    third = [
        push(
            stack_buf.at[place.stack_index],
            stack_buf.at[place.stack_index],
            sems.at[2, 0, step],
            sems.at[2, 1, step],
            place.in_stack(step),
        )
        for step in range(1, 2 * place.nm)
    ]
    meanwhile[2]()
    for copy in third:
        copy.wait_recv()
    return first + second + third


PANEL = 4


def eliminate(gram, cross):
    size, lanes = cross.shape
    rows = lax.broadcasted_iota(jnp.int32, (size, lanes), 0)
    scale = jnp.ones((size, lanes), jnp.float32)
    for first in range(0, size, PANEL):
        columns = [
            jnp.broadcast_to(gram[:, k : k + 1], (size, lanes)) for k in range(first, first + PANEL)
        ]
        for at in range(PANEL):
            k = first + at
            inverse = 1.0 / columns[at][k : k + 1]
            factor = jnp.where(rows == k, 0.0, columns[at] * inverse)
            scale = jnp.where(rows == k, inverse, scale)
            for later in range(at + 1, PANEL):
                columns[later] = columns[later] - factor * columns[later][k : k + 1]
            cross = cross - factor * cross[k : k + 1]
            gram = gram - factor * gram[k : k + 1]
    return cross * scale


def ahead(values, axis):
    return pltpu.roll(values, values.shape[axis] - 1, axis)


def behind(values, axis):
    return pltpu.roll(values, 1, axis)


def flux(cells, plane, field, direction, pressure, normal):
    value = cells[field, plane]
    if field == RHO:
        return cells[MOM + direction, plane], value
    if field == ENERGY:
        return (value + pressure) * normal, value
    result = value * normal
    return (result + pressure if field == MOM + direction else result), value


def first_faces(cells, faces, plane, fields):
    low_v, high_v = cells[VEL, plane], cells[VEL, plane + 1]
    low_p, high_p = cells[PRES, plane], cells[PRES, plane + 1]
    speed = jnp.maximum(
        jnp.abs(low_v) + cells[SOUND, plane], jnp.abs(high_v) + cells[SOUND, plane + 1]
    )
    for field in fields:
        low_f, low_u = flux(cells, plane, field, 0, low_p, low_v)
        high_f, high_u = flux(cells, plane + 1, field, 0, high_p, high_v)
        faces[CONSERVED.index(field), plane] = (low_f + high_f) - speed * (high_u - low_u)


def changes(cells, faces, plane, fields):
    sums = [faces[CONSERVED.index(f), plane] - faces[CONSERVED.index(f), plane - 1] for f in fields]
    pressure, sound = cells[PRES, plane], cells[SOUND, plane]
    for direction in (1, 2):
        axis = direction - 1
        normal = cells[VEL + direction, plane]
        speed = jnp.abs(normal) + sound
        speed = jnp.maximum(speed, ahead(speed, axis))
        for at, field in enumerate(fields):
            here, value = flux(cells, plane, field, direction, pressure, normal)
            face = (here + ahead(here, axis)) - speed * (ahead(value, axis) - value)
            sums[at] = sums[at] + (face - behind(face, axis))
    return sums


def complete_initial(cells, plane, rows):
    rho, pressure = cells[RHO, plane, rows], cells[PRES, plane, rows]
    squares = None
    for k in range(3):
        velocity = cells[VEL + k, plane, rows]
        cells[MOM + k, plane, rows] = rho * velocity
        squares = velocity * velocity if squares is None else squares + velocity * velocity
    cells[ENERGY, plane, rows] = pressure * (1.0 / (HEAT_RATIO - 1.0)) + 0.5 * rho * squares
    cells[SOUND, plane, rows] = jnp.sqrt(HEAT_RATIO * pressure / rho)


def first_stage(cells, faces, after, plane):
    sums = changes(cells, faces, plane, CONSERVED)
    values = [cells[f, plane] - HALF_STEP * s for f, s in zip(CONSERVED, sums)]
    rho, energy = values[0], values[4]
    inverse = 1.0 / rho
    kinetic = None
    for k in range(3):
        velocity = values[1 + k] * inverse
        after[MOM + k, plane] = values[1 + k]
        after[VEL + k, plane] = velocity
        term = values[1 + k] * velocity
        kinetic = term if kinetic is None else kinetic + term
    pressure = (HEAT_RATIO - 1.0) * (energy - 0.5 * kinetic)
    after[RHO, plane] = rho
    after[ENERGY, plane] = energy
    after[PRES, plane] = pressure
    after[SOUND, plane] = jnp.sqrt(HEAT_RATIO * pressure * inverse)


def second_stage(cells, after, faces, result, plane, fields):
    sums = changes(after, faces, plane, fields)
    for field, s in zip(fields, sums):
        value = 0.5 * cells[field, plane] + 0.5 * (after[field, plane] - HALF_STEP * s)
        result[CONSERVED.index(field), plane - 2] = value[:OWN_ROWS]


def over(first, stop, body):
    lax.fori_loop(first, stop, lambda i, carry: (body(i), carry)[1], 0)


def window_kernel(
    nz, ny, nm, density, velocity, pressure, block, test, state, out,
    cells, after, faces, result, row_send, row_recv, corner_send, corner_recv, pick, thin,
    block_in, test_in,
    matrix_all, fold_half, fold_plane, fold_z, fold_all, prod_half, prod_plane, prod_z, prod_all,
    local_sems, halo_sems, sems, member_sems,
):
    place = Place(nz, ny, nm)
    rank = block.shape[2]
    snaps = block.shape[1]
    barrier = pltpu.get_barrier_semaphore()
    peers = place.everyone()
    own = pl.ds(0, OWN_ROWS)
    loads = [
        pltpu.make_async_copy(density.at[0], cells.at[RHO, 2:6, own], local_sems.at[0]),
        pltpu.make_async_copy(velocity.at[0], cells.at[VEL : VEL + 3, 2:6, own], local_sems.at[1]),
        pltpu.make_async_copy(pressure.at[0], cells.at[PRES, 2:6, own], local_sems.at[2]),
    ]
    late_loads = [
        pltpu.make_async_copy(block.at[0], block_in, local_sems.at[3]),
        pltpu.make_async_copy(test, test_in, local_sems.at[4]),
    ]
    for copy in loads + late_loads:
        copy.start()
    for device in peers:
        pl.semaphore_signal(barrier, inc=1, device_id=device, device_id_type=MESH)
    row = lax.broadcasted_iota(jnp.int32, pick.shape, 0)
    column = lax.broadcasted_iota(jnp.int32, pick.shape, 1)
    pick[...] = jnp.where(row == 2 * column, 1.0, 0.0) - jnp.where(row % 2 == 0, 1.0 / snaps, 0.0)
    for copy in loads:
        copy.wait()
    raw = slice(0, 5)
    for i in range(4):
        row_send[0, :, 2 * i : 2 * i + 2] = cells[raw, 2 + i, OWN_ROWS - 2 : OWN_ROWS]
        row_send[1, :, 2 * i : 2 * i + 2] = cells[raw, 2 + i, 0:2]
    corners = ((1, 1), (1, -1), (-1, 1), (-1, -1))
    for at, (up_x, up_y) in enumerate(corners):
        line = OWN_ROWS - 1 if up_y == 1 else 0
        for f in range(5):
            corner_send[at, f : f + 1] = cells[f, 5 if up_x == 1 else 2, line : line + 1]
    pl.semaphore_wait(barrier, len(peers))

    def plane_push(index, source, target, up_x):
        return push(
            cells.at[raw, source, own],
            cells.at[raw, target, own],
            halo_sems.at[0, index],
            halo_sems.at[1, index],
            place.neighbour(up_x, 0),
        )

    up_near, down_near = plane_push(0, 5, 1, 1), plane_push(1, 2, 6, -1)
    row_copies = [
        push(
            row_send.at[i],
            row_recv.at[i],
            halo_sems.at[0, 2 + i],
            halo_sems.at[1, 2 + i],
            place.neighbour(0, 1 - 2 * i),
        )
        for i in range(2)
    ]
    corner_copies = [
        push(
            corner_send.at[i],
            corner_recv.at[i],
            halo_sems.at[0, 4 + i],
            halo_sems.at[1, 4 + i],
            place.neighbour(*corners[i]),
        )
        for i in range(4)
    ]
    up_far, down_far = plane_push(8, 4, 0, 1), plane_push(9, 3, 7, -1)
    sent = [up_near, down_near, *row_copies, *corner_copies, up_far, down_far]

    over(2, 6, lambda p: complete_initial(cells, p, own))
    halo = pl.ds(OWN_ROWS, ROWS - OWN_ROWS)
    for copy in row_copies:
        copy.wait_recv()
    for i in range(4):
        cells[raw, 2 + i, ROWS - 2 : ROWS] = row_recv[0, :, 2 * i : 2 * i + 2]
        cells[raw, 2 + i, OWN_ROWS : OWN_ROWS + 2] = row_recv[1, :, 2 * i : 2 * i + 2]
    over(2, 6, lambda p: complete_initial(cells, p, halo))
    over(2, 5, lambda p: first_faces(cells, faces, p, CONSERVED))
    over(3, 5, lambda p: first_stage(cells, faces, after, p))

    for copy in corner_copies:
        copy.wait_recv()
    for at, (up_x, up_y) in enumerate(corners):
        line = ROWS - 1 if up_y == 1 else OWN_ROWS
        for f in range(5):
            cells[f, 1 if up_x == 1 else 6, line : line + 1] = corner_recv[at, f : f + 1]
    everything = pl.ds(0, ROWS)
    for copy, near, face, inner in ((down_near, 6, 5, 5), (up_near, 1, 1, 2)):
        copy.wait_recv()
        complete_initial(cells, near, everything)
        first_faces(cells, faces, face, CONSERVED)
        first_stage(cells, faces, after, inner)
    mass = (RHO,)
    rest = CONSERVED[1:]
    over(2, 5, lambda p: first_faces(after, faces, p, mass))
    second_stage(cells, after, faces, result, 4, mass)
    up_far.wait_recv()
    complete_initial(cells, 0, everything)
    first_faces(cells, faces, 0, CONSERVED)
    first_stage(cells, faces, after, 1)
    first_faces(after, faces, 1, mass)
    second_stage(cells, after, faces, result, 2, mass)

    even = pl.ds(0, OWN_ROWS // 2, stride=2)
    for i in range(2):
        for side in range(2):
            lanes = slice(128 * side, 128 * side + 128)
            thin[2 * i + side] = result[0, 2 * i, :, lanes]
    sampled = jnp.concatenate(
        [jnp.concatenate([thin[2 * i, even], thin[2 * i + 1, even]], axis=1) for i in range(2)],
        axis=0,
    )
    matrix = dot_nn(sampled, pick[...])
    matrix_all[place.m] = matrix
    for copy in late_loads:
        copy.wait()
    fold = dot_nn(dot_nt(block_in[...].T, matrix), matrix)
    fold_half[0] = fold[:8]
    fold_half[1] = fold[8:]
    gathers = [
        push(
            matrix_all.at[place.m],
            matrix_all.at[place.m],
            member_sems.at[0, step],
            member_sems.at[1, step],
            place.same_cells(step),
        )
        for step in range(1, nm)
    ]

    def last_plane():
        down_far.wait_recv()
        complete_initial(cells, 7, everything)
        first_faces(cells, faces, 6, CONSERVED)
        first_stage(cells, faces, after, 6)

    def other_fields():
        first_faces(after, faces, 5, mass)
        second_stage(cells, after, faces, result, 3, mass)
        second_stage(cells, after, faces, result, 5, mass)
        over(1, 6, lambda p: first_faces(after, faces, p, rest))
        over(2, 6, lambda p: second_stage(cells, after, faces, result, p, rest))

    store = pltpu.make_async_copy(result, state.at[0], local_sems.at[5])

    def nothing():
        pass

    sent += reduce_and_gather(
        place, fold_half, fold_plane, fold_z, fold_all, sems.at[0],
        (last_plane, other_fields, store.start),
    )
    for copy in gathers:
        copy.wait_recv()
    bases_t = [
        dot_nt(jnp.concatenate([fold_all[2 * i], fold_all[2 * i + 1]], axis=0), matrix_all[i])
        for i in range(nm)
    ]
    stacked_t = jnp.concatenate(bases_t, axis=0)
    own_fold = jnp.concatenate([fold_all[2 * place.m], fold_all[2 * place.m + 1]], axis=0)
    own_t = dot_nt(own_fold, matrix)
    wide = jnp.concatenate(
        [stacked_t, jnp.zeros((128 - nm * rank, stacked_t.shape[1]), jnp.float32)], axis=0
    )
    gram_rows = dot_nt(own_t, wide)
    vectors = jnp.concatenate([test_in[0], test_in[1]], axis=0)
    cross_rows = dot_nn(own_t, vectors)
    for core in range(2):
        prod_half[core, :, :128] = gram_rows[8 * core : 8 * core + 8]
        prod_half[core, :, 128:] = cross_rows[8 * core : 8 * core + 8]
    sent += reduce_and_gather(
        place, prod_half, prod_plane, prod_z, prod_all, sems.at[1], (nothing, nothing, nothing)
    )
    both = jnp.concatenate([prod_all[i] for i in range(2 * nm)], axis=0)
    weights = eliminate(both[:, :128], both[:, 128:])
    projected = dot_nn(stacked_t.T, weights)
    half = projected.shape[0] // 2
    out[0] = projected[:half]
    out[1] = projected[half:]
    store.wait()
    for copy in sent + gathers:
        copy.wait_send()


def shards(sizes, density, velocity, pressure, start_block, test_vectors):
    nz, ny, nm = sizes
    slots = max(2 * ny, nz, 2 * nm)
    anywhere = pl.BlockSpec(memory_space=pl.ANY)
    f32 = jnp.float32
    samples = test_vectors.shape[0] * test_vectors.shape[1]
    return pl.pallas_call(
        functools.partial(window_kernel, nz, ny, nm),
        out_shape=(
            jax.ShapeDtypeStruct((1, 5, *density.shape[1:]), f32),
            jax.ShapeDtypeStruct(test_vectors.shape, f32),
        ),
        in_specs=[anywhere] * 5,
        out_specs=(anywhere, pl.BlockSpec(memory_space=pltpu.VMEM)),
        scratch_shapes=[
            pltpu.VMEM((10, PLANES, ROWS, 256), f32),
            pltpu.VMEM((10, PLANES, ROWS, 256), f32),
            pltpu.VMEM((5, PLANES, ROWS, 256), f32),
            pltpu.VMEM((5, 4, OWN_ROWS, 256), f32),
            pltpu.VMEM((2, 5, 8, 256), f32),
            pltpu.VMEM((2, 5, 8, 256), f32),
            pltpu.VMEM((4, 8, 256), f32),
            pltpu.VMEM((4, 8, 256), f32),
            pltpu.VMEM((256, 128), f32),
            pltpu.VMEM((4, OWN_ROWS, 128), f32),
            pltpu.VMEM(start_block.shape[1:], f32),
            pltpu.VMEM(test_vectors.shape, f32),
            pltpu.VMEM((nm, samples, 128), f32),
            pltpu.VMEM((2, 8, 128), f32),
            pltpu.VMEM((2 * ny, 8, 128), f32),
            pltpu.VMEM((nz, 8, 128), f32),
            pltpu.VMEM((2 * nm, 8, 128), f32),
            pltpu.VMEM((2, 8, 256), f32),
            pltpu.VMEM((2 * ny, 8, 256), f32),
            pltpu.VMEM((nz, 8, 256), f32),
            pltpu.VMEM((2 * nm, 8, 256), f32),
            pltpu.SemaphoreType.DMA((6,)),
            pltpu.SemaphoreType.DMA((2, 10)),
            pltpu.SemaphoreType.DMA((2, 3, 2, slots)),
            pltpu.SemaphoreType.DMA((2, nm)),
        ],
        compiler_params=pltpu.CompilerParams(
            collective_id=0, has_side_effects=True, vmem_limit_bytes=48 * 1024 * 1024
        ),
    )(density, velocity, pressure, start_block, test_vectors)


def solution(mesh):
    sizes = (mesh.shape["gx"] // 2, mesh.shape["gy"], mesh.shape["member"])
    return jax.shard_map(
        functools.partial(shards, sizes),
        mesh=mesh,
        in_specs=(
            P("member", "gx", "gy", None),
            P("member", None, "gx", "gy", None),
            P("member", "gx", "gy", None),
            P("member", None, None),
            P("gx", "gy", None),
        ),
        out_specs=(P("member", None, "gx", "gy", None), P("gx", "gy", None)),
        check_vma=False,
    )
```

```python
import functools

import jax
import jax.numpy as jnp
from jax import lax
from jax.experimental import pallas as pl
from jax.experimental.pallas import tpu as pltpu
from jax.sharding import PartitionSpec as P

HEAT_RATIO = 1.4
TIME_STEP = 0.08
HALF_STEP = 0.5 * TIME_STEP
PRECISE = lax.Precision.HIGHEST
MESH = pl.DeviceIdType.MESH

PLANES, ROWS, OWN_ROWS = 8, 40, 32
RHO, VEL, PRES, MOM, ENERGY, SOUND = 0, 1, 4, 5, 8, 9
CONSERVED = (RHO, MOM, MOM + 1, MOM + 2, ENERGY)


def dot_nt(left, right):
    return lax.dot_general(
        left, right, (((1,), (1,)), ((), ())), precision=PRECISE, preferred_element_type=jnp.float32
    )


def dot_nn(left, right):
    return lax.dot_general(
        left, right, (((1,), (0,)), ((), ())), precision=PRECISE, preferred_element_type=jnp.float32
    )


class Place:
    def __init__(self, nz, ny, nm):
        self.nz, self.ny, self.nm = nz, ny, nm
        self.gx = lax.axis_index("gx")
        self.gy = lax.axis_index("gy")
        self.m = lax.axis_index("member")
        self.z = self.gx // 2
        self.c = self.gx % 2
        self.plane_index = self.gy * 2 + self.c
        self.stack_index = self.m * 2 + self.c

    def neighbour(self, up_x, up_y):
        nx = 2 * self.nz
        return ((self.gx + up_x + nx) % nx, (self.gy + up_y + self.ny) % self.ny, self.m)

    def in_plane(self, step):
        other = (self.plane_index + step) % (2 * self.ny)
        return other % 2, (2 * self.z + other % 2, other // 2, self.m)

    def along_z(self, step):
        return (2 * ((self.z + step) % self.nz) + self.c, self.gy, self.m)

    def in_stack(self, step):
        other = (self.stack_index + step) % (2 * self.nm)
        return (2 * self.z + other % 2, self.gy, other // 2)

    def same_cells(self, step):
        return (self.gx, self.gy, (self.m + step) % self.nm)

    def everyone(self):
        peers = [self.neighbour(x, y) for x in (-1, 0, 1) for y in (-1, 0, 1) if (x, y) != (0, 0)]
        peers += [self.in_plane(step)[1] for step in range(1, 2 * self.ny)]
        peers += [self.along_z(step) for step in range(1, self.nz)]
        peers += [self.in_stack(step) for step in range(1, 2 * self.nm)]
        return peers


def push(src, dst, send_sem, recv_sem, device):
    copy = pltpu.make_async_remote_copy(
        src_ref=src,
        dst_ref=dst,
        send_sem=send_sem,
        recv_sem=recv_sem,
        device_id=device,
        device_id_type=MESH,
    )
    copy.start()
    return copy


def total(buffer, count):
    values = [buffer[i] for i in range(count)]
    while len(values) > 1:
        pairs = [a + b for a, b in zip(values[::2], values[1::2])]
        values = pairs + ([values[-1]] if len(values) % 2 else [])
    return values[0]


def reduce_and_gather(place, halves, plane_buf, z_buf, stack_buf, sems, meanwhile):
    first = []
    for step in range(1, 2 * place.ny):
        core, device = place.in_plane(step)
        first.append(
            push(
                halves.at[core],
                plane_buf.at[place.plane_index],
                sems.at[0, 0, step],
                sems.at[0, 1, step],
                device,
            )
        )
    plane_buf[place.plane_index] = halves[place.c]
    meanwhile[0]()
    for copy in first:
        copy.wait_recv()
    z_buf[place.z] = total(plane_buf, 2 * place.ny)
    second = [
        push(
            z_buf.at[place.z],
            z_buf.at[place.z],
            sems.at[1, 0, step],
            sems.at[1, 1, step],
            place.along_z(step),
        )
        for step in range(1, place.nz)
    ]
    meanwhile[1]()
    for copy in second:
        copy.wait_recv()
    stack_buf[place.stack_index] = total(z_buf, place.nz)
    third = [
        push(
            stack_buf.at[place.stack_index],
            stack_buf.at[place.stack_index],
            sems.at[2, 0, step],
            sems.at[2, 1, step],
            place.in_stack(step),
        )
        for step in range(1, 2 * place.nm)
    ]
    meanwhile[2]()
    for copy in third:
        copy.wait_recv()
    return first + second + third


PANEL = 8


def eliminate(gram, cross):
    size, lanes = cross.shape
    rows = lax.broadcasted_iota(jnp.int32, (size, lanes), 0)
    scale = jnp.ones((size, lanes), jnp.float32)
    for first in range(0, size, PANEL):
        columns = [
            jnp.broadcast_to(gram[:, k : k + 1], (size, lanes)) for k in range(first, first + PANEL)
        ]
        for at in range(PANEL):
            k = first + at
            inverse = 1.0 / columns[at][k : k + 1]
            factor = jnp.where(rows == k, 0.0, columns[at] * inverse)
            scale = jnp.where(rows == k, inverse, scale)
            for later in range(at + 1, PANEL):
                columns[later] = columns[later] - factor * columns[later][k : k + 1]
            cross = cross - factor * cross[k : k + 1]
            gram = gram - factor * gram[k : k + 1]
    return cross * scale


def ahead(values, axis):
    return pltpu.roll(values, values.shape[axis] - 1, axis)


def behind(values, axis):
    return pltpu.roll(values, 1, axis)


def flux(cells, plane, field, direction, pressure, normal):
    value = cells[field, plane]
    if field == RHO:
        return cells[MOM + direction, plane], value
    if field == ENERGY:
        return (value + pressure) * normal, value
    result = value * normal
    return (result + pressure if field == MOM + direction else result), value


def first_faces(cells, faces, plane, fields):
    low_v, high_v = cells[VEL, plane], cells[VEL, plane + 1]
    low_p, high_p = cells[PRES, plane], cells[PRES, plane + 1]
    speed = jnp.maximum(
        jnp.abs(low_v) + cells[SOUND, plane], jnp.abs(high_v) + cells[SOUND, plane + 1]
    )
    for field in fields:
        low_f, low_u = flux(cells, plane, field, 0, low_p, low_v)
        high_f, high_u = flux(cells, plane + 1, field, 0, high_p, high_v)
        faces[CONSERVED.index(field), plane] = (low_f + high_f) - speed * (high_u - low_u)


def changes(cells, faces, plane, fields):
    sums = [faces[CONSERVED.index(f), plane] - faces[CONSERVED.index(f), plane - 1] for f in fields]
    pressure, sound = cells[PRES, plane], cells[SOUND, plane]
    for direction in (1, 2):
        axis = direction - 1
        normal = cells[VEL + direction, plane]
        speed = jnp.abs(normal) + sound
        speed = jnp.maximum(speed, ahead(speed, axis))
        for at, field in enumerate(fields):
            here, value = flux(cells, plane, field, direction, pressure, normal)
            face = (here + ahead(here, axis)) - speed * (ahead(value, axis) - value)
            sums[at] = sums[at] + (face - behind(face, axis))
    return sums


def complete_initial(cells, plane, rows):
    rho, pressure = cells[RHO, plane, rows], cells[PRES, plane, rows]
    squares = None
    for k in range(3):
        velocity = cells[VEL + k, plane, rows]
        cells[MOM + k, plane, rows] = rho * velocity
        squares = velocity * velocity if squares is None else squares + velocity * velocity
    cells[ENERGY, plane, rows] = pressure * (1.0 / (HEAT_RATIO - 1.0)) + 0.5 * rho * squares
    cells[SOUND, plane, rows] = jnp.sqrt(HEAT_RATIO * pressure / rho)


def first_stage(cells, faces, after, plane):
    sums = changes(cells, faces, plane, CONSERVED)
    values = [cells[f, plane] - HALF_STEP * s for f, s in zip(CONSERVED, sums)]
    rho, energy = values[0], values[4]
    inverse = 1.0 / rho
    kinetic = None
    for k in range(3):
        velocity = values[1 + k] * inverse
        after[MOM + k, plane] = values[1 + k]
        after[VEL + k, plane] = velocity
        term = values[1 + k] * velocity
        kinetic = term if kinetic is None else kinetic + term
    pressure = (HEAT_RATIO - 1.0) * (energy - 0.5 * kinetic)
    after[RHO, plane] = rho
    after[ENERGY, plane] = energy
    after[PRES, plane] = pressure
    after[SOUND, plane] = jnp.sqrt(HEAT_RATIO * pressure * inverse)


def second_stage(cells, after, faces, result, plane, fields):
    sums = changes(after, faces, plane, fields)
    for field, s in zip(fields, sums):
        value = 0.5 * cells[field, plane] + 0.5 * (after[field, plane] - HALF_STEP * s)
        result[CONSERVED.index(field), plane - 2] = value[:OWN_ROWS]


def over(first, stop, body):
    lax.fori_loop(first, stop, lambda i, carry: (body(i), carry)[1], 0)


def window_kernel(
    nz, ny, nm, density, velocity, pressure, block, test, state, out,
    cells, after, faces, result, row_send, row_recv, corner_send, corner_recv, pick, thin,
    block_in, test_in,
    matrix_all, fold_half, fold_plane, fold_z, fold_all, prod_half, prod_plane, prod_z, prod_all,
    local_sems, halo_sems, sems, member_sems,
):
    place = Place(nz, ny, nm)
    rank = block.shape[2]
    snaps = block.shape[1]
    barrier = pltpu.get_barrier_semaphore()
    peers = place.everyone()
    own = pl.ds(0, OWN_ROWS)
    loads = [
        pltpu.make_async_copy(density.at[0], cells.at[RHO, 2:6, own], local_sems.at[0]),
        pltpu.make_async_copy(velocity.at[0], cells.at[VEL : VEL + 3, 2:6, own], local_sems.at[1]),
        pltpu.make_async_copy(pressure.at[0], cells.at[PRES, 2:6, own], local_sems.at[2]),
    ]
    late_loads = [
        pltpu.make_async_copy(block.at[0], block_in, local_sems.at[3]),
        pltpu.make_async_copy(test, test_in, local_sems.at[4]),
    ]
    for copy in loads + late_loads:
        copy.start()
    for device in peers:
        pl.semaphore_signal(barrier, inc=1, device_id=device, device_id_type=MESH)
    row = lax.broadcasted_iota(jnp.int32, pick.shape, 0)
    column = lax.broadcasted_iota(jnp.int32, pick.shape, 1)
    pick[...] = jnp.where(row == 2 * column, 1.0, 0.0) - jnp.where(row % 2 == 0, 1.0 / snaps, 0.0)
    for copy in loads:
        copy.wait()
    raw = slice(0, 5)
    for i in range(4):
        row_send[0, :, 2 * i : 2 * i + 2] = cells[raw, 2 + i, OWN_ROWS - 2 : OWN_ROWS]
        row_send[1, :, 2 * i : 2 * i + 2] = cells[raw, 2 + i, 0:2]
    corners = ((1, 1), (1, -1), (-1, 1), (-1, -1))
    for at, (up_x, up_y) in enumerate(corners):
        line = OWN_ROWS - 1 if up_y == 1 else 0
        for f in range(5):
            corner_send[at, f : f + 1] = cells[f, 5 if up_x == 1 else 2, line : line + 1]
    pl.semaphore_wait(barrier, len(peers))

    def plane_push(index, source, target, up_x):
        return push(
            cells.at[raw, source, own],
            cells.at[raw, target, own],
            halo_sems.at[0, index],
            halo_sems.at[1, index],
            place.neighbour(up_x, 0),
        )

    up_near, down_near = plane_push(0, 5, 1, 1), plane_push(1, 2, 6, -1)
    row_copies = [
        push(
            row_send.at[i],
            row_recv.at[i],
            halo_sems.at[0, 2 + i],
            halo_sems.at[1, 2 + i],
            place.neighbour(0, 1 - 2 * i),
        )
        for i in range(2)
    ]
    corner_copies = [
        push(
            corner_send.at[i],
            corner_recv.at[i],
            halo_sems.at[0, 4 + i],
            halo_sems.at[1, 4 + i],
            place.neighbour(*corners[i]),
        )
        for i in range(4)
    ]
    up_far, down_far = plane_push(8, 4, 0, 1), plane_push(9, 3, 7, -1)
    sent = [up_near, down_near, *row_copies, *corner_copies, up_far, down_far]

    over(2, 6, lambda p: complete_initial(cells, p, own))
    halo = pl.ds(OWN_ROWS, ROWS - OWN_ROWS)
    for copy in row_copies:
        copy.wait_recv()
    for i in range(4):
        cells[raw, 2 + i, ROWS - 2 : ROWS] = row_recv[0, :, 2 * i : 2 * i + 2]
        cells[raw, 2 + i, OWN_ROWS : OWN_ROWS + 2] = row_recv[1, :, 2 * i : 2 * i + 2]
    over(2, 6, lambda p: complete_initial(cells, p, halo))
    over(2, 5, lambda p: first_faces(cells, faces, p, CONSERVED))
    over(3, 5, lambda p: first_stage(cells, faces, after, p))

    for copy in corner_copies:
        copy.wait_recv()
    for at, (up_x, up_y) in enumerate(corners):
        line = ROWS - 1 if up_y == 1 else OWN_ROWS
        for f in range(5):
            cells[f, 1 if up_x == 1 else 6, line : line + 1] = corner_recv[at, f : f + 1]
    everything = pl.ds(0, ROWS)
    for copy, near, face, inner in ((down_near, 6, 5, 5), (up_near, 1, 1, 2)):
        copy.wait_recv()
        complete_initial(cells, near, everything)
        first_faces(cells, faces, face, CONSERVED)
        first_stage(cells, faces, after, inner)
    mass = (RHO,)
    rest = CONSERVED[1:]
    over(2, 5, lambda p: first_faces(after, faces, p, mass))
    second_stage(cells, after, faces, result, 4, mass)
    up_far.wait_recv()
    complete_initial(cells, 0, everything)
    first_faces(cells, faces, 0, CONSERVED)
    first_stage(cells, faces, after, 1)
    first_faces(after, faces, 1, mass)
    second_stage(cells, after, faces, result, 2, mass)

    even = pl.ds(0, OWN_ROWS // 2, stride=2)
    for i in range(2):
        for side in range(2):
            lanes = slice(128 * side, 128 * side + 128)
            thin[2 * i + side] = result[0, 2 * i, :, lanes]
    sampled = jnp.concatenate(
        [jnp.concatenate([thin[2 * i, even], thin[2 * i + 1, even]], axis=1) for i in range(2)],
        axis=0,
    )
    matrix = dot_nn(sampled, pick[...])
    matrix_all[place.m] = matrix
    for copy in late_loads:
        copy.wait()
    fold = dot_nn(dot_nt(block_in[...].T, matrix), matrix)
    fold_half[0] = fold[:8]
    fold_half[1] = fold[8:]
    gathers = [
        push(
            matrix_all.at[place.m],
            matrix_all.at[place.m],
            member_sems.at[0, step],
            member_sems.at[1, step],
            place.same_cells(step),
        )
        for step in range(1, nm)
    ]

    def last_plane():
        down_far.wait_recv()
        complete_initial(cells, 7, everything)
        first_faces(cells, faces, 6, CONSERVED)
        first_stage(cells, faces, after, 6)

    def other_fields():
        first_faces(after, faces, 5, mass)
        second_stage(cells, after, faces, result, 3, mass)
        second_stage(cells, after, faces, result, 5, mass)
        over(1, 6, lambda p: first_faces(after, faces, p, rest))
        over(2, 6, lambda p: second_stage(cells, after, faces, result, p, rest))

    store = pltpu.make_async_copy(result, state.at[0], local_sems.at[5])

    def nothing():
        pass

    sent += reduce_and_gather(
        place, fold_half, fold_plane, fold_z, fold_all, sems.at[0],
        (last_plane, other_fields, store.start),
    )
    for copy in gathers:
        copy.wait_recv()
    bases_t = [
        dot_nt(jnp.concatenate([fold_all[2 * i], fold_all[2 * i + 1]], axis=0), matrix_all[i])
        for i in range(nm)
    ]
    stacked_t = jnp.concatenate(bases_t, axis=0)
    own_fold = jnp.concatenate([fold_all[2 * place.m], fold_all[2 * place.m + 1]], axis=0)
    own_t = dot_nt(own_fold, matrix)
    wide = jnp.concatenate(
        [stacked_t, jnp.zeros((128 - nm * rank, stacked_t.shape[1]), jnp.float32)], axis=0
    )
    gram_rows = dot_nt(own_t, wide)
    vectors = jnp.concatenate([test_in[0], test_in[1]], axis=0)
    cross_rows = dot_nn(own_t, vectors)
    for core in range(2):
        prod_half[core, :, :128] = gram_rows[8 * core : 8 * core + 8]
        prod_half[core, :, 128:] = cross_rows[8 * core : 8 * core + 8]
    sent += reduce_and_gather(
        place, prod_half, prod_plane, prod_z, prod_all, sems.at[1], (nothing, nothing, nothing)
    )
    both = jnp.concatenate([prod_all[i] for i in range(2 * nm)], axis=0)
    weights = eliminate(both[:, :128], both[:, 128:])
    projected = dot_nn(stacked_t.T, weights)
    half = projected.shape[0] // 2
    out[0] = projected[:half]
    out[1] = projected[half:]
    store.wait()
    for copy in sent + gathers:
        copy.wait_send()


def shards(sizes, density, velocity, pressure, start_block, test_vectors):
    nz, ny, nm = sizes
    slots = max(2 * ny, nz, 2 * nm)
    anywhere = pl.BlockSpec(memory_space=pl.ANY)
    f32 = jnp.float32
    samples = test_vectors.shape[0] * test_vectors.shape[1]
    return pl.pallas_call(
        functools.partial(window_kernel, nz, ny, nm),
        out_shape=(
            jax.ShapeDtypeStruct((1, 5, *density.shape[1:]), f32),
            jax.ShapeDtypeStruct(test_vectors.shape, f32),
        ),
        in_specs=[anywhere] * 5,
        out_specs=(anywhere, pl.BlockSpec(memory_space=pltpu.VMEM)),
        scratch_shapes=[
            pltpu.VMEM((10, PLANES, ROWS, 256), f32),
            pltpu.VMEM((10, PLANES, ROWS, 256), f32),
            pltpu.VMEM((5, PLANES, ROWS, 256), f32),
            pltpu.VMEM((5, 4, OWN_ROWS, 256), f32),
            pltpu.VMEM((2, 5, 8, 256), f32),
            pltpu.VMEM((2, 5, 8, 256), f32),
            pltpu.VMEM((4, 8, 256), f32),
            pltpu.VMEM((4, 8, 256), f32),
            pltpu.VMEM((256, 128), f32),
            pltpu.VMEM((4, OWN_ROWS, 128), f32),
            pltpu.VMEM(start_block.shape[1:], f32),
            pltpu.VMEM(test_vectors.shape, f32),
            pltpu.VMEM((nm, samples, 128), f32),
            pltpu.VMEM((2, 8, 128), f32),
            pltpu.VMEM((2 * ny, 8, 128), f32),
            pltpu.VMEM((nz, 8, 128), f32),
            pltpu.VMEM((2 * nm, 8, 128), f32),
            pltpu.VMEM((2, 8, 256), f32),
            pltpu.VMEM((2 * ny, 8, 256), f32),
            pltpu.VMEM((nz, 8, 256), f32),
            pltpu.VMEM((2 * nm, 8, 256), f32),
            pltpu.SemaphoreType.DMA((6,)),
            pltpu.SemaphoreType.DMA((2, 10)),
            pltpu.SemaphoreType.DMA((2, 3, 2, slots)),
            pltpu.SemaphoreType.DMA((2, nm)),
        ],
        compiler_params=pltpu.CompilerParams(
            collective_id=0, has_side_effects=True, vmem_limit_bytes=48 * 1024 * 1024
        ),
    )(density, velocity, pressure, start_block, test_vectors)


def solution(mesh):
    sizes = (mesh.shape["gx"] // 2, mesh.shape["gy"], mesh.shape["member"])
    return jax.shard_map(
        functools.partial(shards, sizes),
        mesh=mesh,
        in_specs=(
            P("member", "gx", "gy", None),
            P("member", None, "gx", "gy", None),
            P("member", "gx", "gy", None),
            P("member", None, None),
            P("gx", "gy", None),
        ),
        out_specs=(P("member", None, "gx", "gy", None), P("gx", "gy", None)),
        check_vma=False,
    )
```
